32 devices in a mesh: bx: 4 (over y, x), by: 8 (over z, core).
Axes of the slice: x: 2, y: 2, z: 4, core: 2. Of those that a mesh axis runs over, the one named last changes fastest.
Arguments:
- speed_vectors: float32 [3, 6, 60, 120, 128], P(None, None, 'bx', 'by'), may hold values from -10 to 10, as said below
- bin_population: int32 [60, 120, 128], P('bx', 'by'), may hold values from 0 to 6, as said below
- spin_choice: int32 [12, 60, 120, 128], P(None, 'bx', 'by'), may hold values from 0 to 5
- approval_flags: int32 [12, 60, 120, 128], P(None, 'bx', 'by'), may hold values 0 or 1
- round_evenness: int32 [12], replicated, may hold values from 0 to 1
- grid_displacements: int32 [12], replicated, may hold values from 0 to 127
- thermostat_heat_level: float32 [12], replicated, may hold values from 0.5 to 2
Outputs:
- final_velocity: float32 [3, 6, 60, 120, 128], P(None, None, 'bx', 'by')
The draws below stay inside these ranges and needn't reach their ends.
Inputs may be any that keep to these rules, and one draw needn't show every extreme that they name: `bin_population`: A cell's particles fill its first slots. `speed_vectors`: entries in slots at or beyond a cell's occupancy are not read.
All inputs are finite; a program needn't handle non-finite values. No bound on the sum of `approval_flags` on one device may be relied on, other than what follows from the above.
Results may differ from the reference program's by a relative error of at most 0.0003.
Values sent between devices are 32-bit elements; how exact they have to be, the bound alone decides.
A program may use at most 64 MiB of HBM per device.

```python
import math
import jax
import jax.numpy as jnp
from jax import lax

SLOTS = 6
NZ = 128
ROUNDS = 6
ENCOUNTER_ROUNDS = 12
NX = 60
NY = 120


def draw_speed_vectors(key, part):
    key_noise, key_rough, key_flow = jax.random.split(jax.random.fold_in(key, 11), 3)
    shape = (3, SLOTS, NX, NY, NZ)
    xgrid = (jnp.arange(NX, dtype=jnp.float32) + 0.5) / NX
    ygrid = (jnp.arange(NY, dtype=jnp.float32) + 0.5) / NY
    rough = jax.random.uniform(key_rough, (NX, NY, NZ), jnp.float32, 0.5, 1.5)
    flowing = 0.7 * jax.random.normal(key_flow, (3, 1, NX, NY, NZ), jnp.float32)
    noise = jax.random.normal(key_noise, shape, jnp.float32)
    profile = (0.6 + 1.2 * xgrid)[:, None, None] + 0.0 * ygrid[None, :, None]
    values = noise * (profile * rough)[None, None] + flowing
    return jnp.clip(values, -10.0, 10.0).astype(jnp.float32)


def draw_bin_population(key, part):
    xgrid = jnp.arange(NX, dtype=jnp.int32)
    banded = (5 * xgrid // NX)[:, None, None]
    return jax.random.randint(jax.random.fold_in(key, 23), (NX, NY, NZ), banded, banded + 3).astype(jnp.int32)


def with_ends(array, key, low, top_value):
    extent = array.shape
    place = [jax.random.randint(jax.random.fold_in(key, axis), (), 0, extent[axis]) for axis in range(len(extent))]
    array = array.at[tuple(place)].set(low)
    longest = extent.index(max(extent))
    place[longest] = (place[longest] + 1) % extent[longest]
    return array.at[tuple(place)].set(top_value)


def setup_inputs(seed: int = 0) -> dict:
    key_list = jax.random.split(jax.random.key(seed), 8)
    speed_vectors = draw_speed_vectors(jax.random.fold_in(key_list[7], 71), 0)
    bin_population = draw_bin_population(jax.random.fold_in(key_list[7], 71), 0)
    spin_choice = with_ends(jax.random.randint(key_list[2], (ENCOUNTER_ROUNDS, NX, NY, NZ), 0, 6), jax.random.fold_in(key_list[2], 1), 0, 5).astype(jnp.int32)
    approval_flags = with_ends((jax.random.randint(key_list[3], (ENCOUNTER_ROUNDS, NX, NY, NZ), 0, 2) < 1).astype(jnp.int32), jax.random.fold_in(key_list[3], 1), 0, 1)
    round_evenness = with_ends(jax.random.randint(key_list[4], (ENCOUNTER_ROUNDS,), 0, 2), jax.random.fold_in(key_list[4], 1), 0, 1).astype(jnp.int32)
    grid_displacements = with_ends(jax.random.randint(key_list[5], (ENCOUNTER_ROUNDS,), 0, NZ), jax.random.fold_in(key_list[5], 1), 0, NZ - 1).astype(jnp.int32)
    thermostat_heat_level = jnp.clip(jnp.exp(jax.random.uniform(key_list[6], (ENCOUNTER_ROUNDS,), jnp.float32, math.log(0.5), math.log(2.0))), 0.5, 2.0)
    return {"speed_vectors": speed_vectors, "bin_population": bin_population, "spin_choice": spin_choice, "approval_flags": approval_flags, "round_evenness": round_evenness, "grid_displacements": grid_displacements, "thermostat_heat_level": thermostat_heat_level}


turn_angle = 130.0 * math.pi / 180.0
drag_gain = 1.0
excess_coupling = 1e-06

def rotate(thermal, spin_choice):
    picked = spin_choice // 2
    unit_axis = [(picked == member).astype(jnp.float32)[None] for member in range(3)]
    sine_term = (math.sin(turn_angle) * (1 - 2 * (spin_choice % 2)).astype(jnp.float32))[None]
    cosine_term = math.cos(turn_angle)
    along_axis = unit_axis[0] * thermal[0] + unit_axis[1] * thermal[1] + unit_axis[2] * thermal[2]
    result = []
    for member in range(3):
        second = (member + 1) % 3
        third_idx = (member + 2) % 3
        cross_term = unit_axis[second] * thermal[third_idx] - unit_axis[third_idx] * thermal[second]
        result.append(cosine_term * thermal[member] + (1.0 - cosine_term) * unit_axis[member] * along_axis + sine_term * cross_term)
    return jnp.stack(result)

def partner_of(values, is_lower, partner_heading):
    return jnp.where(is_lower, jnp.roll(values, -1, partner_heading), jnp.roll(values, 1, partner_heading))

def scatter_bins(speed_vectors, bin_tallies, spin_choice, approval_flags, round_evenness, thermostat_heat_level, overall_work_sum, partner_heading):
    slot_rank = lax.broadcasted_iota(jnp.int32, (speed_vectors.shape[1],) + bin_tallies.shape, 0)
    occupied = (slot_rank < bin_tallies[None]).astype(jnp.float32)
    moment = lax.optimization_barrier(jnp.sum(speed_vectors * occupied[None], axis=1))
    cell_mass = bin_tallies.astype(jnp.float32)
    safe_mass = jnp.maximum(cell_mass, 1.0)
    thermal = (speed_vectors - (moment / safe_mass)[:, None]) * occupied[None]
    accept_bits = approval_flags.astype(jnp.float32)
    coords = lax.broadcasted_iota(jnp.int32, bin_tallies.shape, partner_heading)
    is_lower = (coords - round_evenness) % 2 == 0
    along_moment = moment[partner_heading]
    other_mass = partner_of(cell_mass, is_lower, partner_heading)
    other_moment = partner_of(along_moment, is_lower, partner_heading)
    other_bits = partner_of(accept_bits, is_lower, partner_heading)
    own_speed = along_moment / safe_mass
    other_speed = other_moment / jnp.maximum(other_mass, 1.0)
    closing = jnp.maximum(jnp.where(is_lower, own_speed - other_speed, other_speed - own_speed), 0.0)
    reduced = cell_mass * other_mass / jnp.maximum(cell_mass + other_mass, 1.0)
    transfer = jnp.maximum(accept_bits, other_bits) * reduced * closing * jnp.tanh(drag_gain * closing)
    new_along = along_moment - jnp.where(is_lower, transfer, -transfer)
    moment = jnp.stack([new_along if member == partner_heading else moment[member] for member in range(3)])
    motion_work_sum = jnp.sum(moment * moment / safe_mass) + jnp.sum(thermal * thermal)
    speed_multiplier = jnp.sqrt(3.0 * thermostat_heat_level * overall_work_sum / (motion_work_sum + excess_coupling))
    return speed_multiplier * ((moment / safe_mass)[:, None] * occupied[None] + rotate(thermal, spin_choice))

def reference(speed_vectors, bin_population, spin_choice, approval_flags, round_evenness, grid_displacements, thermostat_heat_level):
    overall_work_sum = jnp.sum(bin_population.astype(jnp.float32))

    def one_round(round_index, carry):
        ensemble_snapshot, bin_tallies = carry
        for displacement_amount in range(2):
            present_round_number = 2 * round_index + displacement_amount
            ensemble_snapshot = scatter_bins(ensemble_snapshot, bin_tallies, spin_choice[present_round_number], approval_flags[present_round_number], round_evenness[present_round_number], thermostat_heat_level[present_round_number], overall_work_sum, displacement_amount)
            shift_by = grid_displacements[present_round_number]
            ensemble_snapshot = jnp.roll(ensemble_snapshot, shift_by, axis=4)
            bin_tallies = jnp.roll(bin_tallies, shift_by, axis=2)
        return (ensemble_snapshot, bin_tallies)
    ensemble_snapshot, bin_tallies = lax.fori_loop(0, ROUNDS, one_round, (speed_vectors, bin_population))
    return ensemble_snapshot
```

```python
import functools
import math

import jax
import jax.numpy as jnp
from jax import lax
from jax.experimental import pallas as pl
from jax.experimental.pallas import tpu as pltpu
from jax.sharding import PartitionSpec as P

MESH = pl.DeviceIdType.MESH
AXES = ("bx", "by")
COS = math.cos(130.0 * math.pi / 180.0)
SIN = math.sin(130.0 * math.pi / 180.0)
EPSILON = 1e-06


def tree_sum(parts):
    parts = list(parts)
    while len(parts) > 1:
        parts = [sum(parts[i : i + 2]) for i in range(0, len(parts), 2)]
    return parts[0]


def column_sum(value):
    return jnp.sum(value, axis=0, keepdims=True)


def kernel(
    sizes,
    v_hbm,
    count_hbm,
    spin_hbm,
    flag_hbm,
    parity,
    displacement,
    heat,
    x_out,
    f_out,
    w,
    spin,
    flag_x,
    flag_y,
    flag_raw,
    count_x,
    count_y,
    p_x,
    p_y,
    p_z,
    p_tmp,
    iq_x,
    iq_y,
    rr_x,
    rr_y,
    closing,
    coupling,
    transfer,
    rows_by,
    rows_bx,
    load_sem,
    halo_send,
    halo_recv,
    by_send,
    by_recv,
    bx_send,
    bx_recv,
):
    n = sizes
    slots = v_hbm.shape[1]
    ex, ey, nz = count_hbm.shape
    extent = (ex, ey)
    rounds = spin_hbm.shape[0] // 2
    me = (lax.axis_index("bx"), lax.axis_index("by"))
    above = tuple(lax.rem(me[a] + 1, n[a]) for a in range(2))
    below = tuple(lax.rem(me[a] + n[a] - 1, n[a]) for a in range(2))
    flag = (flag_x, flag_y)
    count = (count_x, count_y)
    mom = (p_x, p_y)
    iq = (iq_x, iq_y)
    rr = (rr_x, rr_y)

    load_count = pltpu.make_async_copy(count_hbm, count_x.at[pl.ds(1, ex)], load_sem.at[0])
    load_v = [pltpu.make_async_copy(v_hbm.at[c], w.at[c], load_sem.at[1 + c]) for c in range(3)]
    load_fx = pltpu.make_async_copy(flag_hbm.at[:, 0], flag_x.at[:, pl.ds(1, ex)], load_sem.at[4])
    load_fy = pltpu.make_async_copy(flag_hbm.at[:, 1], flag_raw, load_sem.at[5])
    load_spin = pltpu.make_async_copy(spin_hbm, spin, load_sem.at[6])
    for copy in (load_count, load_v[0], load_fx, load_v[1], load_fy, load_v[2], load_spin):
        copy.start()

    barrier = pltpu.get_barrier_semaphore()
    for a in range(2):
        for step in range(1, n[a]):
            pl.semaphore_signal(
                barrier,
                inc=1,
                device_id={AXES[a]: lax.rem(me[a] + step, n[a])},
                device_id_type=MESH,
            )

    def halo(view, a, kind):
        k = 2 * (2 * kind + a)
        return [
            pltpu.make_async_remote_copy(
                src_ref=view(extent[a]),
                dst_ref=view(0),
                send_sem=halo_send.at[k],
                recv_sem=halo_recv.at[k],
                device_id={AXES[a]: above[a]},
                device_id_type=MESH,
            ),
            pltpu.make_async_remote_copy(
                src_ref=view(1),
                dst_ref=view(extent[a] + 1),
                send_sem=halo_send.at[k + 1],
                recv_sem=halo_recv.at[k + 1],
                device_id={AXES[a]: below[a]},
                device_id_type=MESH,
            ),
        ]

    halo_p = [halo(lambda i, a=a: mom[a].at[i], a, 0) for a in range(2)]
    halo_c = [halo(lambda i, a=a: count[a].at[i], a, 1) for a in range(2)]
    halo_f = [halo(lambda i, a=a: flag[a].at[:, i], a, 2) for a in range(2)]

    def start(copies):
        for copy in copies:
            copy.start()

    def finish(copies):
        for copy in copies:
            copy.wait()

    def inverse(counts):
        return 1.0 / jnp.maximum(counts.astype(jnp.float32), 1.0)

    def split_component(c, target, offset):
        def plane(i, acc):
            counts = count_x[i + 1]
            inv = iq_x[i + 1]
            values = [jnp.where(counts > s, w[c, s, i], 0.0) for s in range(slots)]
            moment = tree_sum(values)
            target[i + offset] = moment
            mean = moment * inv
            thermal = [jnp.where(counts > s, values[s] - mean, 0.0) for s in range(slots)]
            for s in range(slots):
                w[c, s, i] = thermal[s]
            heat_part = acc[0] + tree_sum([t * t for t in thermal])
            return heat_part, acc[1] + moment * mean

        zero = jnp.zeros((ey, nz), jnp.float32)
        return lax.fori_loop(0, ex, plane, (zero, zero))

    load_count.wait()
    number = jnp.zeros((ey, nz), jnp.float32)
    for i in range(1, ex + 1):
        iq_x[i] = inverse(count_x[i])
        number = number + count_x[i].astype(jnp.float32)
    load_v[0].wait()
    thermal_0, energy_x = split_component(0, p_x, 1)
    pl.semaphore_wait(barrier, n[0] + n[1] - 2)
    start(halo_p[0])
    start(halo_c[0])
    load_fx.wait()
    start(halo_f[0])
    load_v[1].wait()
    thermal_1, energy_y = split_component(1, p_tmp, 0)
    for y in range(ey):
        p_y[y + 1] = p_tmp[:, y, :]
        count_y[y + 1] = count_x[pl.ds(1, ex), y, :]
    start(halo_p[1])
    start(halo_c[1])
    load_fy.wait()

    def flags_across(r, carry):
        for y in range(ey):
            flag_y[r, y + 1] = flag_raw[r, :, y, :]
        return carry

    lax.fori_loop(0, rounds, flags_across, 0)
    start(halo_f[1])
    load_v[2].wait()
    thermal_2, energy_z = split_component(2, p_z, 0)

    def reduced_masses(a):
        finish(halo_c[a])
        e = extent[a]
        for i in range(0, e + 2):
            iq[a][i] = inverse(count[a][i])
        for b in range(e + 1):
            low = count[a][b].astype(jnp.float32)
            high = count[a][b + 1].astype(jnp.float32)
            rr[a][b] = low * high / jnp.maximum(low + high, 1.0)

    def offset_of(a, t):
        return (me[a] * extent[a] - parity[t]) & 1

    def prepare(a, r, t, shift):
        finish(halo_p[a])
        p = offset_of(a, t)
        back = lax.rem(nz - shift, nz)
        for j in range((extent[a] + 1) // 2):
            low = 2 * j + 1 - p
            high = 2 * j + 2 - p
            closing[j] = jnp.maximum(
                mom[a][low] * iq[a][low] - mom[a][high] * iq[a][high], 0.0
            )
            bits = jnp.maximum(flag[a][r, low], flag[a][r, high]).astype(jnp.float32)
            coupling[j] = pltpu.roll(bits, back, 1) * rr[a][low]

    def rotate(t, shift):
        back = lax.rem(nz - shift, nz)

        def plane(i, carry):
            kind = pltpu.roll(spin[t, i], back, 1)
            axis = kind >> 1
            sine = jnp.where((kind & 1) == 0, SIN, -SIN)
            own = [jnp.where(axis == c, 1.0, COS) for c in range(3)]
            sin = [jnp.where(axis == c, sine, 0.0) for c in range(3)]
            for s in range(slots):
                x, y, z = (w[c, s, i] for c in range(3))
                w[0, s, i] = own[0] * x + (sin[1] * z - sin[2] * y)
                w[1, s, i] = own[1] * y + (sin[2] * x - sin[0] * z)
                w[2, s, i] = own[2] * z + (sin[0] * y - sin[1] * x)
            return carry

        lax.fori_loop(0, ex, plane, 0)

    def exchange(rows, a, slot, send_sem, recv_sem):
        return [
            pltpu.make_async_remote_copy(
                src_ref=rows.at[slot, me[a]],
                dst_ref=rows.at[slot, me[a]],
                send_sem=send_sem,
                recv_sem=recv_sem,
                device_id={AXES[a]: lax.rem(me[a] + step, n[a])},
                device_id_type=MESH,
            )
            for step in range(1, n[a])
        ]

    def await_rows(rows, a, slot, send_sem, recv_sem):
        view = rows.at[slot, pl.ds(0, n[a] - 1)]
        whole = pltpu.make_async_remote_copy(
            src_ref=view,
            dst_ref=view,
            send_sem=send_sem,
            recv_sem=recv_sem,
            device_id={AXES[a]: above[a]},
            device_id_type=MESH,
        )
        whole.wait_recv()
        whole.wait_send()

    def collide(a, t, scale):
        p = offset_of(a, t)
        sign = (2 * p - 1).astype(jnp.float32)
        for j in range((extent[a] + 1) // 2):
            g = scale * closing[j]
            transfer[j] = coupling[j] * g * jnp.tanh(g)
        energy = []
        for i in range(1, extent[a] + 1):
            if i % 2 == 1:
                moved = scale * mom[a][i] + sign * transfer[(i - 1) // 2]
            else:
                moved = scale * mom[a][i] - sign * transfer[i // 2 - 1 + p]
            mom[a][i] = moved
            energy.append(moved * moved * iq[a][i])
        return column_sum(tree_sum(energy))

    load_spin.wait()
    reduced_masses(0)
    finish(halo_f[0])
    prepare(0, 0, 0, 0)
    number_row = column_sum(number)
    ones = jnp.ones((1, nz), jnp.float32)

    def step(a, r, scales, energies, shift, last_hook):
        t = 2 * r + a
        b = 1 - a
        new_energy = collide(a, t, scales[a])
        partial = new_energy + energies[b] + energies[2]
        rows_by[a, me[1]] = jnp.concatenate([partial, number_row], axis=0)
        start(exchange(rows_by, 1, a, by_send.at[a], by_recv.at[a]))
        if a == 0:

            @pl.when(r > 0)
            def _():
                start(halo_p[1])

        else:

            @pl.when(r < rounds - 1)
            def _():
                start(halo_p[0])

        rotate(t, shift)
        if a == 0:

            @pl.when(r == 0)
            def _():
                reduced_masses(1)
                finish(halo_f[1])

        await_rows(rows_by, 1, a, by_send.at[a], by_recv.at[a])
        rows_bx[a, me[0]] = tree_sum([rows_by[a, i] for i in range(n[1])])
        start(exchange(rows_bx, 0, a, bx_send.at[a], bx_recv.at[a]))
        new_shift = lax.rem(shift + displacement[t], nz)
        if a == 0:
            prepare(1, r, t + 1, new_shift)
        else:

            @pl.when(r < rounds - 1)
            def _():
                prepare(0, r + 1, t + 1, new_shift)

            @pl.when(r == rounds - 1)
            def _():
                last_hook(scales, new_shift)

        await_rows(rows_bx, 0, a, bx_send.at[a], bx_recv.at[a])
        sums = tree_sum([rows_bx[a, i] for i in range(n[0])])
        sums = jnp.sum(sums, axis=1, keepdims=True)
        square = 3.0 * heat[t] * sums[1:2] / (sums[0:1] + EPSILON)
        square = jnp.broadcast_to(square, (1, nz))
        f = jnp.sqrt(square)
        kept = scales[b] * f
        scales = (f, kept, scales[2] * f) if a == 0 else (kept, f, scales[2] * f)
        moved = new_energy * square
        other = energies[b] * square
        pair = (moved, other) if a == 0 else (other, moved)
        return scales, pair + (energies[2] * square,), new_shift, f

    def assemble(scales, shift):
        for y in range(ey):
            p_tmp[:, y, :] = p_y[y + 1]

        def plane(i, carry):
            counts = count_x[i + 1]
            inv = iq_x[i + 1]
            means = (
                scales[0] * (p_x[i + 1] * inv),
                p_tmp[i] * inv,
                scales[2] * (p_z[i] * inv),
            )
            for c in range(3):
                for s in range(slots):
                    value = jnp.where(counts > s, means[c] + scales[2] * w[c, s, i], 0.0)
                    x_out[c, s, i] = pltpu.roll(value, shift, 1)
            return carry

        lax.fori_loop(0, ex, plane, 0)

    def round_body(r, carry):
        scales, energies, shift, _ = carry
        scales, energies, shift, f = step(0, r, scales, energies, shift, None)
        return step(1, r, scales, energies, shift, assemble)

    rest = column_sum(thermal_0 + thermal_1 + thermal_2 + energy_z)
    energies = (column_sum(energy_x), column_sum(energy_y), rest)
    carry = ((ones, ones, ones), energies, jnp.int32(0), ones)
    f_out[...] = lax.fori_loop(0, rounds, round_body, carry)[3]


def per_device(sizes, v, counts, spin, flags, parity, displacement, heat):
    slots = v.shape[1]
    ex, ey, nz = counts.shape
    steps = spin.shape[0]
    rounds = steps // 2
    bonds = (max(ex, ey) + 1) // 2
    assert ex % 2 == 1 and ey % 2 == 1 and ex == ey
    f32, i32 = jnp.float32, jnp.int32
    anywhere = pl.BlockSpec(memory_space=pltpu.HBM)
    scalar = pl.BlockSpec(memory_space=pltpu.SMEM)
    vector = pl.BlockSpec(memory_space=pltpu.VMEM)
    dma = pltpu.SemaphoreType.DMA
    x, f = pl.pallas_call(
        functools.partial(kernel, sizes),
        out_shape=(
            jax.ShapeDtypeStruct(v.shape, f32),
            jax.ShapeDtypeStruct((1, nz), f32),
        ),
        in_specs=[anywhere] * 4 + [scalar] * 3,
        out_specs=(vector, vector),
        scratch_shapes=[
            pltpu.VMEM(v.shape, f32),
            pltpu.VMEM(spin.shape, i32),
            pltpu.VMEM((rounds, ex + 2, ey, nz), i32),
            pltpu.VMEM((rounds, ey + 2, ex, nz), i32),
            pltpu.VMEM((rounds, ex, ey, nz), i32),
            pltpu.VMEM((ex + 2, ey, nz), i32),
            pltpu.VMEM((ey + 2, ex, nz), i32),
            pltpu.VMEM((ex + 2, ey, nz), f32),
            pltpu.VMEM((ey + 2, ex, nz), f32),
            pltpu.VMEM((ex, ey, nz), f32),
            pltpu.VMEM((ex, ey, nz), f32),
            pltpu.VMEM((ex + 2, ey, nz), f32),
            pltpu.VMEM((ey + 2, ex, nz), f32),
            pltpu.VMEM((ex + 1, ey, nz), f32),
            pltpu.VMEM((ey + 1, ex, nz), f32),
            pltpu.VMEM((bonds, ey, nz), f32),
            pltpu.VMEM((bonds, ey, nz), f32),
            pltpu.VMEM((bonds, ey, nz), f32),
            pltpu.VMEM((2, sizes[1], 2, nz), f32),
            pltpu.VMEM((2, sizes[0], 2, nz), f32),
            dma((7,)),
            dma((12,)),
            dma((12,)),
            dma((2,)),
            dma((2,)),
            dma((2,)),
            dma((2,)),
        ],
        compiler_params=pltpu.CompilerParams(
            collective_id=0, has_side_effects=True, vmem_limit_bytes=40 * 2**20
        ),
    )(
        v,
        counts,
        spin,
        flags.reshape((rounds, 2) + flags.shape[1:]),
        parity,
        displacement,
        heat,
    )
    return x * f[0]


def solution(mesh):
    sizes = (mesh.shape["bx"], mesh.shape["by"])
    cells = P(None, "bx", "by", None)
    return jax.shard_map(
        functools.partial(per_device, sizes),
        mesh=mesh,
        in_specs=(
            P(None, None, "bx", "by", None),
            P("bx", "by", None),
            cells,
            cells,
            P(),
            P(),
            P(),
        ),
        out_specs=P(None, None, "bx", "by", None),
        check_vma=False,
    )
```

```python
import functools
import math

import jax
import jax.numpy as jnp
from jax import lax
from jax.experimental import pallas as pl
from jax.experimental.pallas import tpu as pltpu
from jax.sharding import PartitionSpec as P

MESH = pl.DeviceIdType.MESH
AXES = ("bx", "by")
COS = math.cos(130.0 * math.pi / 180.0)
SIN = math.sin(130.0 * math.pi / 180.0)
EPSILON = 1e-06


def tree_sum(parts):
    parts = list(parts)
    while len(parts) > 1:
        parts = [sum(parts[i : i + 2]) for i in range(0, len(parts), 2)]
    return parts[0]


def column_sum(value):
    return jnp.sum(value, axis=0, keepdims=True)


def kernel(
    sizes,
    v_hbm,
    count_hbm,
    spin_hbm,
    flag_hbm,
    parity_hbm,
    displacement_hbm,
    heat_hbm,
    x_out,
    f_out,
    parity,
    displacement,
    heat,
    w,
    spin,
    flag_x,
    flag_y,
    flag_raw,
    count_x,
    count_y,
    p_x,
    p_y,
    p_z,
    p_tmp,
    iq_x,
    iq_y,
    rr_x,
    rr_y,
    closing,
    coupling,
    transfer,
    rows,
    load_sem,
    halo_send,
    halo_recv,
    row_send,
    row_recv,
):
    n = sizes
    slots = v_hbm.shape[1]
    ex, ey, nz = count_hbm.shape
    extent = (ex, ey)
    rounds = spin_hbm.shape[0] // 2
    me = (lax.axis_index("bx"), lax.axis_index("by"))
    above = tuple(lax.rem(me[a] + 1, n[a]) for a in range(2))
    below = tuple(lax.rem(me[a] + n[a] - 1, n[a]) for a in range(2))
    my_row = me[0] * n[1] + me[1]
    offsets = [(i, j) for i in range(n[0]) for j in range(n[1]) if i or j]
    offsets.sort(key=lambda o: -(min(o[0], n[0] - o[0]) + min(o[1], n[1] - o[1])))
    peers = [(lax.rem(me[0] + i, n[0]), lax.rem(me[1] + j, n[1])) for i, j in offsets]
    flag = (flag_x, flag_y)
    count = (count_x, count_y)
    mom = (p_x, p_y)
    iq = (iq_x, iq_y)
    rr = (rr_x, rr_y)

    load_count = pltpu.make_async_copy(count_hbm, count_x.at[pl.ds(1, ex)], load_sem.at[0])
    load_v = [pltpu.make_async_copy(v_hbm.at[c], w.at[c], load_sem.at[1 + c]) for c in range(3)]
    load_fx = pltpu.make_async_copy(flag_hbm.at[:, 0], flag_x.at[:, pl.ds(1, ex)], load_sem.at[4])
    load_fy = pltpu.make_async_copy(flag_hbm.at[:, 1], flag_raw, load_sem.at[5])
    load_spin = pltpu.make_async_copy(spin_hbm, spin, load_sem.at[6])
    load_scalars = [
        pltpu.make_async_copy(source, target, load_sem.at[7 + i])
        for i, (source, target) in enumerate(
            ((parity_hbm, parity), (displacement_hbm, displacement), (heat_hbm, heat))
        )
    ]
    for copy in load_scalars:
        copy.start()
    for copy in (load_count, load_v[0], load_fx, load_v[1], load_fy, load_v[2], load_spin):
        copy.start()

    barrier = pltpu.get_barrier_semaphore()
    for peer in peers:
        pl.semaphore_signal(barrier, inc=1, device_id=peer, device_id_type=MESH)

    def halo(view, a, kind):
        k = 2 * (2 * kind + a)
        return [
            pltpu.make_async_remote_copy(
                src_ref=view(extent[a]),
                dst_ref=view(0),
                send_sem=halo_send.at[k],
                recv_sem=halo_recv.at[k],
                device_id={AXES[a]: above[a]},
                device_id_type=MESH,
            ),
            pltpu.make_async_remote_copy(
                src_ref=view(1),
                dst_ref=view(extent[a] + 1),
                send_sem=halo_send.at[k + 1],
                recv_sem=halo_recv.at[k + 1],
                device_id={AXES[a]: below[a]},
                device_id_type=MESH,
            ),
        ]

    halo_p = [halo(lambda i, a=a: mom[a].at[i], a, 0) for a in range(2)]
    halo_c = [halo(lambda i, a=a: count[a].at[i], a, 1) for a in range(2)]
    halo_f = [halo(lambda i, a=a: flag[a].at[:, i], a, 2) for a in range(2)]

    def start(copies):
        for copy in copies:
            copy.start()

    def finish(copies):
        for copy in copies:
            copy.wait()

    def inverse(counts):
        return 1.0 / jnp.maximum(counts.astype(jnp.float32), 1.0)

    def split_component(c, target, offset):
        def plane(i, acc):
            counts = count_x[i + 1]
            inv = iq_x[i + 1]
            values = [jnp.where(counts > s, w[c, s, i], 0.0) for s in range(slots)]
            moment = tree_sum(values)
            target[i + offset] = moment
            mean = moment * inv
            thermal = [jnp.where(counts > s, values[s] - mean, 0.0) for s in range(slots)]
            for s in range(slots):
                w[c, s, i] = thermal[s]
            heat_part = acc[0] + tree_sum([t * t for t in thermal])
            return heat_part, acc[1] + moment * mean

        zero = jnp.zeros((ey, nz), jnp.float32)
        return lax.fori_loop(0, ex, plane, (zero, zero))

    load_count.wait()
    number = jnp.zeros((ey, nz), jnp.float32)
    for i in range(1, ex + 1):
        iq_x[i] = inverse(count_x[i])
        number = number + count_x[i].astype(jnp.float32)
    load_v[0].wait()
    thermal_0, energy_x = split_component(0, p_x, 1)
    pl.semaphore_wait(barrier, n[0] * n[1] - 1)
    start(halo_p[0])
    start(halo_c[0])
    load_fx.wait()
    start(halo_f[0])
    load_v[1].wait()
    thermal_1, energy_y = split_component(1, p_tmp, 0)
    for y in range(ey):
        p_y[y + 1] = p_tmp[:, y, :]
        count_y[y + 1] = count_x[pl.ds(1, ex), y, :]
    start(halo_p[1])
    start(halo_c[1])
    load_fy.wait()

    def flags_across(r, carry):
        for y in range(ey):
            flag_y[r, y + 1] = flag_raw[r, :, y, :]
        return carry

    lax.fori_loop(0, rounds, flags_across, 0)
    start(halo_f[1])
    load_v[2].wait()
    thermal_2, energy_z = split_component(2, p_z, 0)

    def reduced_masses(a):
        finish(halo_c[a])
        e = extent[a]
        for i in range(0, e + 2):
            iq[a][i] = inverse(count[a][i])
        for b in range(e + 1):
            low = count[a][b].astype(jnp.float32)
            high = count[a][b + 1].astype(jnp.float32)
            rr[a][b] = low * high / jnp.maximum(low + high, 1.0)

    def offset_of(a, t):
        return (me[a] * extent[a] - parity[t]) & 1

    def prepare(a, r, t, shift):
        finish(halo_p[a])
        p = offset_of(a, t)
        back = lax.rem(nz - shift, nz)
        for j in range((extent[a] + 1) // 2):
            low = 2 * j + 1 - p
            high = 2 * j + 2 - p
            closing[j] = jnp.maximum(
                mom[a][low] * iq[a][low] - mom[a][high] * iq[a][high], 0.0
            )
            bits = jnp.maximum(flag[a][r, low], flag[a][r, high]).astype(jnp.float32)
            coupling[j] = pltpu.roll(bits, back, 1) * rr[a][low]

    def rotate(t, shift):
        back = lax.rem(nz - shift, nz)

        def plane(i, carry):
            kind = pltpu.roll(spin[t, i], back, 1)
            axis = kind >> 1
            sine = jnp.where((kind & 1) == 0, SIN, -SIN)
            own = [jnp.where(axis == c, 1.0, COS) for c in range(3)]
            sin = [jnp.where(axis == c, sine, 0.0) for c in range(3)]
            for s in range(slots):
                x, y, z = (w[c, s, i] for c in range(3))
                w[0, s, i] = own[0] * x + (sin[1] * z - sin[2] * y)
                w[1, s, i] = own[1] * y + (sin[2] * x - sin[0] * z)
                w[2, s, i] = own[2] * z + (sin[0] * y - sin[1] * x)
            return carry

        lax.fori_loop(0, ex, plane, 0)

    def exchange(a):
        return [
            pltpu.make_async_remote_copy(
                src_ref=rows.at[a, my_row],
                dst_ref=rows.at[a, my_row],
                send_sem=row_send.at[a],
                recv_sem=row_recv.at[a],
                device_id=peer,
                device_id_type=MESH,
            )
            for peer in peers
        ]

    def await_rows(a):
        view = rows.at[a, pl.ds(0, n[0] * n[1] - 1)]
        whole = pltpu.make_async_remote_copy(
            src_ref=view,
            dst_ref=view,
            send_sem=row_send.at[a],
            recv_sem=row_recv.at[a],
            device_id=peers[0],
            device_id_type=MESH,
        )
        whole.wait_recv()
        whole.wait_send()

    def collide(a, t, scale):
        p = offset_of(a, t)
        sign = (2 * p - 1).astype(jnp.float32)
        for j in range((extent[a] + 1) // 2):
            g = scale * closing[j]
            transfer[j] = coupling[j] * g * jnp.tanh(g)
        energy = []
        for i in range(1, extent[a] + 1):
            if i % 2 == 1:
                moved = scale * mom[a][i] + sign * transfer[(i - 1) // 2]
            else:
                moved = scale * mom[a][i] - sign * transfer[i // 2 - 1 + p]
            mom[a][i] = moved
            energy.append(moved * moved * iq[a][i])
        return column_sum(tree_sum(energy))

    load_spin.wait()
    for copy in load_scalars:
        copy.wait()
    reduced_masses(0)
    finish(halo_f[0])
    prepare(0, 0, 0, 0)
    number_row = column_sum(number)
    ones = jnp.ones((1, nz), jnp.float32)

    def step(a, r, scales, energies, shift, last_hook):
        t = 2 * r + a
        b = 1 - a
        new_energy = collide(a, t, scales[a])
        partial = new_energy + energies[b] + energies[2]
        rows[a, my_row] = jnp.concatenate([partial, number_row], axis=0)
        start(exchange(a))
        if a == 0:

            @pl.when(r > 0)
            def _():
                start(halo_p[1])

        else:

            @pl.when(r < rounds - 1)
            def _():
                start(halo_p[0])

        rotate(t, shift)
        if a == 0:

            @pl.when(r == 0)
            def _():
                reduced_masses(1)
                finish(halo_f[1])

        new_shift = lax.rem(shift + displacement[t], nz)
        if a == 0:
            prepare(1, r, t + 1, new_shift)
        else:

            @pl.when(r < rounds - 1)
            def _():
                prepare(0, r + 1, t + 1, new_shift)

            @pl.when(r == rounds - 1)
            def _():
                last_hook(scales, new_shift)

        await_rows(a)
        sums = tree_sum([rows[a, i] for i in range(n[0] * n[1])])
        sums = jnp.sum(sums, axis=1, keepdims=True)
        square = 3.0 * heat[t] * sums[1:2] / (sums[0:1] + EPSILON)
        square = jnp.broadcast_to(square, (1, nz))
        f = jnp.sqrt(square)
        kept = scales[b] * f
        scales = (f, kept, scales[2] * f) if a == 0 else (kept, f, scales[2] * f)
        moved = new_energy * square
        other = energies[b] * square
        pair = (moved, other) if a == 0 else (other, moved)
        return scales, pair + (energies[2] * square,), new_shift, f

    def assemble(scales, shift):
        for y in range(ey):
            p_tmp[:, y, :] = p_y[y + 1]

        def plane(i, carry):
            counts = count_x[i + 1]
            inv = iq_x[i + 1]
            means = (
                scales[0] * (p_x[i + 1] * inv),
                p_tmp[i] * inv,
                scales[2] * (p_z[i] * inv),
            )
            for c in range(3):
                for s in range(slots):
                    value = jnp.where(counts > s, means[c] + scales[2] * w[c, s, i], 0.0)
                    x_out[c, s, i] = pltpu.roll(value, shift, 1)
            return carry

        lax.fori_loop(0, ex, plane, 0)

    def round_body(r, carry):
        scales, energies, shift, _ = carry
        scales, energies, shift, f = step(0, r, scales, energies, shift, None)
        return step(1, r, scales, energies, shift, assemble)

    rest = column_sum(thermal_0 + thermal_1 + thermal_2 + energy_z)
    energies = (column_sum(energy_x), column_sum(energy_y), rest)
    carry = ((ones, ones, ones), energies, jnp.int32(0), ones)
    f_out[...] = lax.fori_loop(0, rounds, round_body, carry)[3]


def per_device(sizes, v, counts, spin, flags, parity, displacement, heat):
    slots = v.shape[1]
    ex, ey, nz = counts.shape
    steps = spin.shape[0]
    rounds = steps // 2
    bonds = (max(ex, ey) + 1) // 2
    assert ex % 2 == 1 and ey % 2 == 1 and ex == ey
    f32, i32 = jnp.float32, jnp.int32
    anywhere = pl.BlockSpec(memory_space=pltpu.HBM)
    vector = pl.BlockSpec(memory_space=pltpu.VMEM)
    dma = pltpu.SemaphoreType.DMA
    x, f = pl.pallas_call(
        functools.partial(kernel, sizes),
        out_shape=(
            jax.ShapeDtypeStruct(v.shape, f32),
            jax.ShapeDtypeStruct((1, nz), f32),
        ),
        in_specs=[anywhere] * 7,
        out_specs=(vector, vector),
        scratch_shapes=[
            pltpu.SMEM(parity.shape, i32),
            pltpu.SMEM(displacement.shape, i32),
            pltpu.SMEM(heat.shape, f32),
            pltpu.VMEM(v.shape, f32),
            pltpu.VMEM(spin.shape, i32),
            pltpu.VMEM((rounds, ex + 2, ey, nz), i32),
            pltpu.VMEM((rounds, ey + 2, ex, nz), i32),
            pltpu.VMEM((rounds, ex, ey, nz), i32),
            pltpu.VMEM((ex + 2, ey, nz), i32),
            pltpu.VMEM((ey + 2, ex, nz), i32),
            pltpu.VMEM((ex + 2, ey, nz), f32),
            pltpu.VMEM((ey + 2, ex, nz), f32),
            pltpu.VMEM((ex, ey, nz), f32),
            pltpu.VMEM((ex, ey, nz), f32),
            pltpu.VMEM((ex + 2, ey, nz), f32),
            pltpu.VMEM((ey + 2, ex, nz), f32),
            pltpu.VMEM((ex + 1, ey, nz), f32),
            pltpu.VMEM((ey + 1, ex, nz), f32),
            pltpu.VMEM((bonds, ey, nz), f32),
            pltpu.VMEM((bonds, ey, nz), f32),
            pltpu.VMEM((bonds, ey, nz), f32),
            pltpu.VMEM((2, sizes[0] * sizes[1], 2, nz), f32),
            dma((10,)),
            dma((12,)),
            dma((12,)),
            dma((2,)),
            dma((2,)),
        ],
        compiler_params=pltpu.CompilerParams(
            collective_id=0, has_side_effects=True, vmem_limit_bytes=40 * 2**20
        ),
    )(
        *(
            pltpu.with_memory_space_constraint(value, pltpu.HBM)
            for value in (
                v,
                counts,
                spin,
                flags.reshape((rounds, 2) + flags.shape[1:]),
                parity,
                displacement,
                heat,
            )
        )
    )
    return x * f[0]


def solution(mesh):
    sizes = (mesh.shape["bx"], mesh.shape["by"])
    cells = P(None, "bx", "by", None)
    return jax.shard_map(
        functools.partial(per_device, sizes),
        mesh=mesh,
        in_specs=(
            P(None, None, "bx", "by", None),
            P("bx", "by", None),
            cells,
            cells,
            P(),
            P(),
            P(),
        ),
        out_specs=P(None, None, "bx", "by", None),
        check_vma=False,
    )
```

```python
import functools
import math

import jax
import jax.numpy as jnp
from jax import lax
from jax.experimental import pallas as pl
from jax.experimental.pallas import tpu as pltpu
from jax.sharding import PartitionSpec as P

MESH = pl.DeviceIdType.MESH
AXES = ("bx", "by")
COS = math.cos(130.0 * math.pi / 180.0)
SIN = math.sin(130.0 * math.pi / 180.0)
EPSILON = 1e-06


def tree_sum(parts):
    parts = list(parts)
    while len(parts) > 1:
        parts = [sum(parts[i : i + 2]) for i in range(0, len(parts), 2)]
    return parts[0]


def column_sum(value):
    return jnp.sum(value, axis=0, keepdims=True)


def kernel(
    sizes,
    v_hbm,
    count_hbm,
    spin_hbm,
    flag_hbm,
    parity_hbm,
    displacement_hbm,
    heat_hbm,
    x_out,
    f_out,
    parity,
    displacement,
    heat,
    w,
    spin,
    flag_x,
    flag_y,
    flag_raw,
    count_x,
    count_y,
    p_x,
    p_y,
    p_z,
    p_tmp,
    iq_x,
    iq_y,
    rr_x,
    rr_y,
    closing,
    coupling,
    transfer,
    rows,
    load_sem,
    halo_send,
    halo_recv,
    row_send,
    row_recv,
    numbers,
    number_send,
    number_recv,
    total,
):
    n = sizes
    slots = v_hbm.shape[1]
    ex, ey, nz = count_hbm.shape
    extent = (ex, ey)
    rounds = spin_hbm.shape[0] // 2
    me = (lax.axis_index("bx"), lax.axis_index("by"))
    above = tuple(lax.rem(me[a] + 1, n[a]) for a in range(2))
    below = tuple(lax.rem(me[a] + n[a] - 1, n[a]) for a in range(2))
    my_row = me[0] * n[1] + me[1]
    offsets = [(i, j) for i in range(n[0]) for j in range(n[1]) if i or j]
    offsets.sort(key=lambda o: -(min(o[0], n[0] - o[0]) + min(o[1], n[1] - o[1])))
    peers = [(lax.rem(me[0] + i, n[0]), lax.rem(me[1] + j, n[1])) for i, j in offsets]
    flag = (flag_x, flag_y)
    count = (count_x, count_y)
    mom = (p_x, p_y)
    iq = (iq_x, iq_y)
    rr = (rr_x, rr_y)

    load_count = pltpu.make_async_copy(count_hbm, count_x.at[pl.ds(1, ex)], load_sem.at[0])
    load_v = [pltpu.make_async_copy(v_hbm.at[c], w.at[c], load_sem.at[1 + c]) for c in range(3)]
    load_fx = pltpu.make_async_copy(flag_hbm.at[:, 0], flag_x.at[:, pl.ds(1, ex)], load_sem.at[4])
    load_fy = pltpu.make_async_copy(flag_hbm.at[:, 1], flag_raw, load_sem.at[5])
    load_spin = pltpu.make_async_copy(spin_hbm, spin, load_sem.at[6])
    load_scalars = [
        pltpu.make_async_copy(source, target, load_sem.at[7 + i])
        for i, (source, target) in enumerate(
            ((parity_hbm, parity), (displacement_hbm, displacement), (heat_hbm, heat))
        )
    ]
    for copy in load_scalars:
        copy.start()
    for copy in (load_count, load_v[0], load_fx, load_v[1], load_fy, load_v[2], load_spin):
        copy.start()

    barrier = pltpu.get_barrier_semaphore()
    for peer in peers:
        pl.semaphore_signal(barrier, inc=1, device_id=peer, device_id_type=MESH)

    def halo(view, a, kind):
        k = 2 * (2 * kind + a)
        return [
            pltpu.make_async_remote_copy(
                src_ref=view(extent[a]),
                dst_ref=view(0),
                send_sem=halo_send.at[k],
                recv_sem=halo_recv.at[k],
                device_id={AXES[a]: above[a]},
                device_id_type=MESH,
            ),
            pltpu.make_async_remote_copy(
                src_ref=view(1),
                dst_ref=view(extent[a] + 1),
                send_sem=halo_send.at[k + 1],
                recv_sem=halo_recv.at[k + 1],
                device_id={AXES[a]: below[a]},
                device_id_type=MESH,
            ),
        ]

    halo_p = [halo(lambda i, a=a: mom[a].at[i], a, 0) for a in range(2)]
    halo_c = [halo(lambda i, a=a: count[a].at[i], a, 1) for a in range(2)]
    halo_f = [halo(lambda i, a=a: flag[a].at[:, i], a, 2) for a in range(2)]

    def start(copies):
        for copy in copies:
            copy.start()

    def finish(copies):
        for copy in copies:
            copy.wait()

    def inverse(counts):
        return 1.0 / jnp.maximum(counts.astype(jnp.float32), 1.0)

    def exchange(a, rows=rows, row_send=row_send, row_recv=row_recv):
        return [
            pltpu.make_async_remote_copy(
                src_ref=rows.at[a, my_row],
                dst_ref=rows.at[a, my_row],
                send_sem=row_send.at[a],
                recv_sem=row_recv.at[a],
                device_id=peer,
                device_id_type=MESH,
            )
            for peer in peers
        ]

    def await_rows(a, rows=rows, row_send=row_send, row_recv=row_recv):
        view = rows.at[a, pl.ds(0, n[0] * n[1] - 1)]
        whole = pltpu.make_async_remote_copy(
            src_ref=view,
            dst_ref=view,
            send_sem=row_send.at[a],
            recv_sem=row_recv.at[a],
            device_id=peers[0],
            device_id_type=MESH,
        )
        whole.wait_recv()
        whole.wait_send()

    def split_component(c, target, offset):
        def plane(i, acc):
            counts = count_x[i + 1]
            inv = iq_x[i + 1]
            values = [jnp.where(counts > s, w[c, s, i], 0.0) for s in range(slots)]
            moment = tree_sum(values)
            target[i + offset] = moment
            mean = moment * inv
            thermal = [jnp.where(counts > s, values[s] - mean, 0.0) for s in range(slots)]
            for s in range(slots):
                w[c, s, i] = thermal[s]
            heat_part = acc[0] + tree_sum([t * t for t in thermal])
            return heat_part, acc[1] + moment * mean

        zero = jnp.zeros((ey, nz), jnp.float32)
        return lax.fori_loop(0, ex, plane, (zero, zero))

    load_count.wait()
    number = jnp.zeros((ey, nz), jnp.float32)
    for i in range(1, ex + 1):
        iq_x[i] = inverse(count_x[i])
        number = number + count_x[i].astype(jnp.float32)
    load_v[0].wait()
    thermal_0, energy_x = split_component(0, p_x, 1)
    pl.semaphore_wait(barrier, n[0] * n[1] - 1)
    start(halo_p[0])
    start(halo_c[0])
    load_fx.wait()
    start(halo_f[0])
    numbers[0, my_row] = column_sum(number)
    start(exchange(0, numbers, number_send, number_recv))
    load_v[1].wait()
    thermal_1, energy_y = split_component(1, p_tmp, 0)
    for y in range(ey):
        p_y[y + 1] = p_tmp[:, y, :]
        count_y[y + 1] = count_x[pl.ds(1, ex), y, :]
    start(halo_p[1])
    start(halo_c[1])
    load_fy.wait()

    def flags_across(r, carry):
        for y in range(ey):
            flag_y[r, y + 1] = flag_raw[r, :, y, :]
        return carry

    lax.fori_loop(0, rounds, flags_across, 0)
    start(halo_f[1])
    load_v[2].wait()
    thermal_2, energy_z = split_component(2, p_z, 0)

    def reduced_masses(a):
        finish(halo_c[a])
        e = extent[a]
        for i in range(0, e + 2):
            iq[a][i] = inverse(count[a][i])
        for b in range(e + 1):
            low = count[a][b].astype(jnp.float32)
            high = count[a][b + 1].astype(jnp.float32)
            rr[a][b] = low * high / jnp.maximum(low + high, 1.0)

    def offset_of(a, t):
        return (me[a] * extent[a] - parity[t]) & 1

    def prepare(a, r, t, shift):
        finish(halo_p[a])
        p = offset_of(a, t)
        back = lax.rem(nz - shift, nz)
        for j in range((extent[a] + 1) // 2):
            low = 2 * j + 1 - p
            high = 2 * j + 2 - p
            closing[j] = jnp.maximum(
                mom[a][low] * iq[a][low] - mom[a][high] * iq[a][high], 0.0
            )
            bits = jnp.maximum(flag[a][r, low], flag[a][r, high]).astype(jnp.float32)
            coupling[j] = pltpu.roll(bits, back, 1) * rr[a][low]

    def rotate(t, shift):
        back = lax.rem(nz - shift, nz)

        def plane(i, carry):
            kind = pltpu.roll(spin[t, i], back, 1)
            axis = kind >> 1
            sine = jnp.where((kind & 1) == 0, SIN, -SIN)
            own = [jnp.where(axis == c, 1.0, COS) for c in range(3)]
            sin = [jnp.where(axis == c, sine, 0.0) for c in range(3)]
            for s in range(slots):
                x, y, z = (w[c, s, i] for c in range(3))
                w[0, s, i] = own[0] * x + (sin[1] * z - sin[2] * y)
                w[1, s, i] = own[1] * y + (sin[2] * x - sin[0] * z)
                w[2, s, i] = own[2] * z + (sin[0] * y - sin[1] * x)
            return carry

        lax.fori_loop(0, ex, plane, 0)

    def collide(a, t, scale):
        p = offset_of(a, t)
        sign = (2 * p - 1).astype(jnp.float32)
        for j in range((extent[a] + 1) // 2):
            g = scale * closing[j]
            transfer[j] = coupling[j] * g * jnp.tanh(g)
        energy = []
        for i in range(1, extent[a] + 1):
            if i % 2 == 1:
                moved = scale * mom[a][i] + sign * transfer[(i - 1) // 2]
            else:
                moved = scale * mom[a][i] - sign * transfer[i // 2 - 1 + p]
            mom[a][i] = moved
            energy.append(moved * moved * iq[a][i])
        return column_sum(tree_sum(energy))

    load_spin.wait()
    for copy in load_scalars:
        copy.wait()
    reduced_masses(0)
    finish(halo_f[0])
    prepare(0, 0, 0, 0)
    ones = jnp.ones((1, nz), jnp.float32)

    def step(a, r, scales, energies, shift, last_hook):
        t = 2 * r + a
        b = 1 - a
        new_energy = collide(a, t, scales[a])
        partial = new_energy + energies[b] + energies[2]
        rows[a, my_row] = partial
        start(exchange(a))
        if a == 0:

            @pl.when(r > 0)
            def _():
                start(halo_p[1])

        else:

            @pl.when(r < rounds - 1)
            def _():
                start(halo_p[0])

        rotate(t, shift)
        if a == 0:

            @pl.when(r == 0)
            def _():
                reduced_masses(1)
                finish(halo_f[1])
                await_rows(0, numbers, number_send, number_recv)
                everyone = tree_sum([numbers[0, i] for i in range(n[0] * n[1])])
                everyone = jnp.sum(everyone, axis=1, keepdims=True)
                total[...] = jnp.broadcast_to(everyone, (1, nz))

        new_shift = lax.rem(shift + displacement[t], nz)
        if a == 0:
            prepare(1, r, t + 1, new_shift)
        else:

            @pl.when(r < rounds - 1)
            def _():
                prepare(0, r + 1, t + 1, new_shift)

            @pl.when(r == rounds - 1)
            def _():
                last_hook(scales, new_shift)

        await_rows(a)
        sums = tree_sum([rows[a, i] for i in range(n[0] * n[1])])
        sums = jnp.sum(sums, axis=1, keepdims=True)
        kinetic = jnp.broadcast_to(sums, (1, nz))
        square = (3.0 * heat[t]) * total[...] / (kinetic + EPSILON)
        f = jnp.sqrt(square)
        kept = scales[b] * f
        scales = (f, kept, scales[2] * f) if a == 0 else (kept, f, scales[2] * f)
        moved = new_energy * square
        other = energies[b] * square
        pair = (moved, other) if a == 0 else (other, moved)
        return scales, pair + (energies[2] * square,), new_shift, f

    def assemble(scales, shift):
        for y in range(ey):
            p_tmp[:, y, :] = p_y[y + 1]

        def plane(i, carry):
            counts = count_x[i + 1]
            inv = iq_x[i + 1]
            means = (
                scales[0] * (p_x[i + 1] * inv),
                p_tmp[i] * inv,
                scales[2] * (p_z[i] * inv),
            )
            for c in range(3):
                for s in range(slots):
                    value = jnp.where(counts > s, means[c] + scales[2] * w[c, s, i], 0.0)
                    x_out[c, s, i] = pltpu.roll(value, shift, 1)
            return carry

        lax.fori_loop(0, ex, plane, 0)

    def round_body(r, carry):
        scales, energies, shift, _ = carry
        scales, energies, shift, f = step(0, r, scales, energies, shift, None)
        return step(1, r, scales, energies, shift, assemble)

    rest = column_sum(thermal_0 + thermal_1 + thermal_2 + energy_z)
    energies = (column_sum(energy_x), column_sum(energy_y), rest)
    carry = ((ones, ones, ones), energies, jnp.int32(0), ones)
    f_out[...] = lax.fori_loop(0, rounds, round_body, carry)[3]


def per_device(sizes, v, counts, spin, flags, parity, displacement, heat):
    slots = v.shape[1]
    ex, ey, nz = counts.shape
    steps = spin.shape[0]
    rounds = steps // 2
    bonds = (max(ex, ey) + 1) // 2
    assert ex % 2 == 1 and ey % 2 == 1 and ex == ey
    f32, i32 = jnp.float32, jnp.int32
    anywhere = pl.BlockSpec(memory_space=pltpu.HBM)
    vector = pl.BlockSpec(memory_space=pltpu.VMEM)
    dma = pltpu.SemaphoreType.DMA
    x, f = pl.pallas_call(
        functools.partial(kernel, sizes),
        out_shape=(
            jax.ShapeDtypeStruct(v.shape, f32),
            jax.ShapeDtypeStruct((1, nz), f32),
        ),
        in_specs=[anywhere] * 7,
        out_specs=(vector, vector),
        scratch_shapes=[
            pltpu.SMEM(parity.shape, i32),
            pltpu.SMEM(displacement.shape, i32),
            pltpu.SMEM(heat.shape, f32),
            pltpu.VMEM(v.shape, f32),
            pltpu.VMEM(spin.shape, i32),
            pltpu.VMEM((rounds, ex + 2, ey, nz), i32),
            pltpu.VMEM((rounds, ey + 2, ex, nz), i32),
            pltpu.VMEM((rounds, ex, ey, nz), i32),
            pltpu.VMEM((ex + 2, ey, nz), i32),
            pltpu.VMEM((ey + 2, ex, nz), i32),
            pltpu.VMEM((ex + 2, ey, nz), f32),
            pltpu.VMEM((ey + 2, ex, nz), f32),
            pltpu.VMEM((ex, ey, nz), f32),
            pltpu.VMEM((ex, ey, nz), f32),
            pltpu.VMEM((ex + 2, ey, nz), f32),
            pltpu.VMEM((ey + 2, ex, nz), f32),
            pltpu.VMEM((ex + 1, ey, nz), f32),
            pltpu.VMEM((ey + 1, ex, nz), f32),
            pltpu.VMEM((bonds, ey, nz), f32),
            pltpu.VMEM((bonds, ey, nz), f32),
            pltpu.VMEM((bonds, ey, nz), f32),
            pltpu.VMEM((2, sizes[0] * sizes[1], 1, nz), f32),
            dma((10,)),
            dma((12,)),
            dma((12,)),
            dma((2,)),
            dma((2,)),
            pltpu.VMEM((1, sizes[0] * sizes[1], 1, nz), f32),
            dma((1,)),
            dma((1,)),
            pltpu.VMEM((1, nz), f32),
        ],
        compiler_params=pltpu.CompilerParams(
            collective_id=0, has_side_effects=True, vmem_limit_bytes=40 * 2**20
        ),
    )(
        *(
            pltpu.with_memory_space_constraint(value, pltpu.HBM)
            for value in (
                v,
                counts,
                spin,
                flags.reshape((rounds, 2) + flags.shape[1:]),
                parity,
                displacement,
                heat,
            )
        )
    )
    return x * f[0]


def solution(mesh):
    sizes = (mesh.shape["bx"], mesh.shape["by"])
    cells = P(None, "bx", "by", None)
    return jax.shard_map(
        functools.partial(per_device, sizes),
        mesh=mesh,
        in_specs=(
            P(None, None, "bx", "by", None),
            P("bx", "by", None),
            cells,
            cells,
            P(),
            P(),
            P(),
        ),
        out_specs=P(None, None, "bx", "by", None),
        check_vma=False,
    )
```

```python
import functools
import math

import jax
import jax.numpy as jnp
from jax import lax
from jax.experimental import pallas as pl
from jax.experimental.pallas import tpu as pltpu
from jax.sharding import PartitionSpec as P

MESH = pl.DeviceIdType.MESH
AXES = ("bx", "by")
COS = math.cos(130.0 * math.pi / 180.0)
SIN = math.sin(130.0 * math.pi / 180.0)
EPSILON = 1e-06


def tree_sum(parts):
    parts = list(parts)
    while len(parts) > 1:
        parts = [sum(parts[i : i + 2]) for i in range(0, len(parts), 2)]
    return parts[0]


def column_sum(value):
    return jnp.sum(value, axis=0, keepdims=True)


def kernel(
    sizes,
    v_hbm,
    count_hbm,
    spin_hbm,
    flag_hbm,
    parity_hbm,
    displacement_hbm,
    heat_hbm,
    x_out,
    f_out,
    parity,
    displacement,
    heat,
    w,
    spin,
    flag_x,
    flag_y,
    flag_raw,
    count_x,
    count_y,
    p_x,
    p_y,
    p_z,
    p_tmp,
    iq_x,
    iq_y,
    rr_x,
    rr_y,
    closing,
    coupling,
    transfer,
    rows,
    load_sem,
    halo_send,
    halo_recv,
    row_send,
    row_recv,
    numbers,
    number_send,
    number_recv,
    total,
):
    n = sizes
    slots = v_hbm.shape[1]
    ex, ey, nz = count_hbm.shape
    extent = (ex, ey)
    rounds = spin_hbm.shape[0] // 2
    me = (lax.axis_index("bx"), lax.axis_index("by"))
    above = tuple(lax.rem(me[a] + 1, n[a]) for a in range(2))
    below = tuple(lax.rem(me[a] + n[a] - 1, n[a]) for a in range(2))
    my_row = me[0] * n[1] + me[1]
    columns = [me[0]]
    if n[0] % 2 == 0:
        half = n[0] // 2
        for i in range(half):
            for k in range(2):
                if i or k:
                    columns.append(
                        2 * lax.rem(me[0] // 2 + i, half) + lax.rem(lax.rem(me[0], 2) + k, 2)
                    )
    else:
        columns += [lax.rem(me[0] + i, n[0]) for i in range(1, n[0])]
    low_half = (2 * me[1]) // n[1] == 0
    peers = []
    for k in range(n[1] - 1):
        down = jnp.where(n[1] - 1 - k > me[1], n[1] - 1 - k, n[1] - 2 - k)
        up = jnp.where(k < me[1], k, k + 1)
        row = jnp.where(low_half, down, up)
        peers += [(column, row) for column in reversed(columns)]
    peers += [(column, me[1]) for column in reversed(columns[1:])]
    flag = (flag_x, flag_y)
    count = (count_x, count_y)
    mom = (p_x, p_y)
    iq = (iq_x, iq_y)
    rr = (rr_x, rr_y)

    load_count = pltpu.make_async_copy(count_hbm, count_x.at[pl.ds(1, ex)], load_sem.at[0])
    load_v = [pltpu.make_async_copy(v_hbm.at[c], w.at[c], load_sem.at[1 + c]) for c in range(3)]
    load_fx = pltpu.make_async_copy(flag_hbm.at[:, 0], flag_x.at[:, pl.ds(1, ex)], load_sem.at[4])
    load_fy = pltpu.make_async_copy(flag_hbm.at[:, 1], flag_raw, load_sem.at[5])
    load_spin = pltpu.make_async_copy(spin_hbm, spin, load_sem.at[6])
    load_scalars = [
        pltpu.make_async_copy(source, target, load_sem.at[7 + i])
        for i, (source, target) in enumerate(
            ((parity_hbm, parity), (displacement_hbm, displacement), (heat_hbm, heat))
        )
    ]
    for copy in load_scalars:
        copy.start()
    for copy in (load_count, load_v[0], load_fx, load_v[1], load_fy, load_v[2], load_spin):
        copy.start()

    barrier = pltpu.get_barrier_semaphore()
    for peer in peers:
        pl.semaphore_signal(barrier, inc=1, device_id=peer, device_id_type=MESH)

    def halo(view, a, kind):
        k = 2 * (2 * kind + a)
        return [
            pltpu.make_async_remote_copy(
                src_ref=view(extent[a]),
                dst_ref=view(0),
                send_sem=halo_send.at[k],
                recv_sem=halo_recv.at[k],
                device_id={AXES[a]: above[a]},
                device_id_type=MESH,
            ),
            pltpu.make_async_remote_copy(
                src_ref=view(1),
                dst_ref=view(extent[a] + 1),
                send_sem=halo_send.at[k + 1],
                recv_sem=halo_recv.at[k + 1],
                device_id={AXES[a]: below[a]},
                device_id_type=MESH,
            ),
        ]

    halo_p = [halo(lambda i, a=a: mom[a].at[i], a, 0) for a in range(2)]
    halo_c = [halo(lambda i, a=a: count[a].at[i], a, 1) for a in range(2)]
    halo_f = [halo(lambda i, a=a: flag[a].at[:, i], a, 2) for a in range(2)]

    def start(copies):
        for copy in copies:
            copy.start()

    def finish(copies):
        for copy in copies:
            copy.wait()

    def inverse(counts):
        return 1.0 / jnp.maximum(counts.astype(jnp.float32), 1.0)

    def exchange(a, rows=rows, row_send=row_send, row_recv=row_recv):
        return [
            pltpu.make_async_remote_copy(
                src_ref=rows.at[a, my_row],
                dst_ref=rows.at[a, my_row],
                send_sem=row_send.at[a],
                recv_sem=row_recv.at[a],
                device_id=peer,
                device_id_type=MESH,
            )
            for peer in peers
        ]

    def await_rows(a, rows=rows, row_send=row_send, row_recv=row_recv):
        view = rows.at[a, pl.ds(0, n[0] * n[1] - 1)]
        whole = pltpu.make_async_remote_copy(
            src_ref=view,
            dst_ref=view,
            send_sem=row_send.at[a],
            recv_sem=row_recv.at[a],
            device_id=peers[0],
            device_id_type=MESH,
        )
        whole.wait_recv()
        whole.wait_send()

    def split_component(c, target, offset):
        def plane(i, acc):
            counts = count_x[i + 1]
            inv = iq_x[i + 1]
            values = [jnp.where(counts > s, w[c, s, i], 0.0) for s in range(slots)]
            moment = tree_sum(values)
            target[i + offset] = moment
            mean = moment * inv
            thermal = [jnp.where(counts > s, values[s] - mean, 0.0) for s in range(slots)]
            for s in range(slots):
                w[c, s, i] = thermal[s]
            heat_part = acc[0] + tree_sum([t * t for t in thermal])
            return heat_part, acc[1] + moment * mean

        zero = jnp.zeros((ey, nz), jnp.float32)
        return lax.fori_loop(0, ex, plane, (zero, zero))

    load_count.wait()
    number = jnp.zeros((ey, nz), jnp.float32)
    for i in range(1, ex + 1):
        iq_x[i] = inverse(count_x[i])
        number = number + count_x[i].astype(jnp.float32)
    load_v[0].wait()
    thermal_0, energy_x = split_component(0, p_x, 1)
    pl.semaphore_wait(barrier, n[0] * n[1] - 1)
    start(halo_p[0])
    start(halo_c[0])
    load_fx.wait()
    start(halo_f[0])
    numbers[0, my_row] = column_sum(number)
    start(exchange(0, numbers, number_send, number_recv))
    load_v[1].wait()
    thermal_1, energy_y = split_component(1, p_tmp, 0)
    for y in range(ey):
        p_y[y + 1] = p_tmp[:, y, :]
        count_y[y + 1] = count_x[pl.ds(1, ex), y, :]
    start(halo_p[1])
    start(halo_c[1])
    load_fy.wait()

    def flags_across(r, carry):
        for y in range(ey):
            flag_y[r, y + 1] = flag_raw[r, :, y, :]
        return carry

    lax.fori_loop(0, rounds, flags_across, 0)
    start(halo_f[1])
    load_v[2].wait()
    thermal_2, energy_z = split_component(2, p_z, 0)

    def reduced_masses(a):
        finish(halo_c[a])
        e = extent[a]
        for i in range(0, e + 2):
            iq[a][i] = inverse(count[a][i])
        for b in range(e + 1):
            low = count[a][b].astype(jnp.float32)
            high = count[a][b + 1].astype(jnp.float32)
            rr[a][b] = low * high / jnp.maximum(low + high, 1.0)

    def offset_of(a, t):
        return (me[a] * extent[a] - parity[t]) & 1

    def prepare(a, r, t, shift):
        finish(halo_p[a])
        p = offset_of(a, t)
        back = lax.rem(nz - shift, nz)
        for j in range((extent[a] + 1) // 2):
            low = 2 * j + 1 - p
            high = 2 * j + 2 - p
            closing[j] = jnp.maximum(
                mom[a][low] * iq[a][low] - mom[a][high] * iq[a][high], 0.0
            )
            bits = jnp.maximum(flag[a][r, low], flag[a][r, high]).astype(jnp.float32)
            coupling[j] = pltpu.roll(bits, back, 1) * rr[a][low]

    def rotate(t, shift):
        back = lax.rem(nz - shift, nz)

        def plane(i, carry):
            kind = pltpu.roll(spin[t, i], back, 1)
            axis = kind >> 1
            sine = jnp.where((kind & 1) == 0, SIN, -SIN)
            own = [jnp.where(axis == c, 1.0, COS) for c in range(3)]
            sin = [jnp.where(axis == c, sine, 0.0) for c in range(3)]
            for s in range(slots):
                x, y, z = (w[c, s, i] for c in range(3))
                w[0, s, i] = own[0] * x + (sin[1] * z - sin[2] * y)
                w[1, s, i] = own[1] * y + (sin[2] * x - sin[0] * z)
                w[2, s, i] = own[2] * z + (sin[0] * y - sin[1] * x)
            return carry

        lax.fori_loop(0, ex, plane, 0)

    def collide(a, t, scale):
        p = offset_of(a, t)
        sign = (2 * p - 1).astype(jnp.float32)
        for j in range((extent[a] + 1) // 2):
            g = scale * closing[j]
            transfer[j] = coupling[j] * g * jnp.tanh(g)
        energy = []
        for i in range(1, extent[a] + 1):
            if i % 2 == 1:
                moved = scale * mom[a][i] + sign * transfer[(i - 1) // 2]
            else:
                moved = scale * mom[a][i] - sign * transfer[i // 2 - 1 + p]
            mom[a][i] = moved
            energy.append(moved * moved * iq[a][i])
        return column_sum(tree_sum(energy))

    load_spin.wait()
    for copy in load_scalars:
        copy.wait()
    reduced_masses(0)
    finish(halo_f[0])
    prepare(0, 0, 0, 0)
    ones = jnp.ones((1, nz), jnp.float32)

    def step(a, r, scales, energies, shift, last_hook):
        t = 2 * r + a
        b = 1 - a
        new_energy = collide(a, t, scales[a])
        partial = new_energy + energies[b] + energies[2]
        rows[a, my_row] = partial
        start(exchange(a))
        if a == 0:

            @pl.when(r > 0)
            def _():
                start(halo_p[1])

        else:

            @pl.when(r < rounds - 1)
            def _():
                start(halo_p[0])

        rotate(t, shift)
        if a == 0:

            @pl.when(r == 0)
            def _():
                reduced_masses(1)
                finish(halo_f[1])
                await_rows(0, numbers, number_send, number_recv)
                everyone = tree_sum([numbers[0, i] for i in range(n[0] * n[1])])
                everyone = jnp.sum(everyone, axis=1, keepdims=True)
                total[...] = jnp.broadcast_to(everyone, (1, nz))

        new_shift = lax.rem(shift + displacement[t], nz)
        if a == 0:
            prepare(1, r, t + 1, new_shift)
        else:

            @pl.when(r < rounds - 1)
            def _():
                prepare(0, r + 1, t + 1, new_shift)

            @pl.when(r == rounds - 1)
            def _():
                last_hook(scales, new_shift)

        await_rows(a)
        sums = tree_sum([rows[a, i] for i in range(n[0] * n[1])])
        sums = jnp.sum(sums, axis=1, keepdims=True)
        kinetic = jnp.broadcast_to(sums, (1, nz))
        f = jnp.sqrt((3.0 * heat[t]) * total[...]) * lax.rsqrt(kinetic + EPSILON)
        square = f * f
        kept = scales[b] * f
        scales = (f, kept, scales[2] * f) if a == 0 else (kept, f, scales[2] * f)
        moved = new_energy * square
        other = energies[b] * square
        pair = (moved, other) if a == 0 else (other, moved)
        return scales, pair + (energies[2] * square,), new_shift, f

    def assemble(scales, shift):
        for y in range(ey):
            p_tmp[:, y, :] = p_y[y + 1]

        def plane(i, carry):
            counts = count_x[i + 1]
            inv = iq_x[i + 1]
            means = (
                scales[0] * (p_x[i + 1] * inv),
                p_tmp[i] * inv,
                scales[2] * (p_z[i] * inv),
            )
            for c in range(3):
                for s in range(slots):
                    value = jnp.where(counts > s, means[c] + scales[2] * w[c, s, i], 0.0)
                    x_out[c, s, i] = pltpu.roll(value, shift, 1)
            return carry

        lax.fori_loop(0, ex, plane, 0)

    def round_body(r, carry):
        scales, energies, shift, _ = carry
        scales, energies, shift, f = step(0, r, scales, energies, shift, None)
        return step(1, r, scales, energies, shift, assemble)

    rest = column_sum(thermal_0 + thermal_1 + thermal_2 + energy_z)
    energies = (column_sum(energy_x), column_sum(energy_y), rest)
    carry = ((ones, ones, ones), energies, jnp.int32(0), ones)
    f_out[...] = lax.fori_loop(0, rounds, round_body, carry)[3]


def per_device(sizes, v, counts, spin, flags, parity, displacement, heat):
    slots = v.shape[1]
    ex, ey, nz = counts.shape
    steps = spin.shape[0]
    rounds = steps // 2
    bonds = (max(ex, ey) + 1) // 2
    assert ex % 2 == 1 and ey % 2 == 1 and ex == ey
    f32, i32 = jnp.float32, jnp.int32
    anywhere = pl.BlockSpec(memory_space=pltpu.HBM)
    vector = pl.BlockSpec(memory_space=pltpu.VMEM)
    dma = pltpu.SemaphoreType.DMA
    x, f = pl.pallas_call(
        functools.partial(kernel, sizes),
        out_shape=(
            jax.ShapeDtypeStruct(v.shape, f32),
            jax.ShapeDtypeStruct((1, nz), f32),
        ),
        in_specs=[anywhere] * 7,
        out_specs=(vector, vector),
        scratch_shapes=[
            pltpu.SMEM(parity.shape, i32),
            pltpu.SMEM(displacement.shape, i32),
            pltpu.SMEM(heat.shape, f32),
            pltpu.VMEM(v.shape, f32),
            pltpu.VMEM(spin.shape, i32),
            pltpu.VMEM((rounds, ex + 2, ey, nz), i32),
            pltpu.VMEM((rounds, ey + 2, ex, nz), i32),
            pltpu.VMEM((rounds, ex, ey, nz), i32),
            pltpu.VMEM((ex + 2, ey, nz), i32),
            pltpu.VMEM((ey + 2, ex, nz), i32),
            pltpu.VMEM((ex + 2, ey, nz), f32),
            pltpu.VMEM((ey + 2, ex, nz), f32),
            pltpu.VMEM((ex, ey, nz), f32),
            pltpu.VMEM((ex, ey, nz), f32),
            pltpu.VMEM((ex + 2, ey, nz), f32),
            pltpu.VMEM((ey + 2, ex, nz), f32),
            pltpu.VMEM((ex + 1, ey, nz), f32),
            pltpu.VMEM((ey + 1, ex, nz), f32),
            pltpu.VMEM((bonds, ey, nz), f32),
            pltpu.VMEM((bonds, ey, nz), f32),
            pltpu.VMEM((bonds, ey, nz), f32),
            pltpu.VMEM((2, sizes[0] * sizes[1], 1, nz), f32),
            dma((10,)),
            dma((12,)),
            dma((12,)),
            dma((2,)),
            dma((2,)),
            pltpu.VMEM((1, sizes[0] * sizes[1], 1, nz), f32),
            dma((1,)),
            dma((1,)),
            pltpu.VMEM((1, nz), f32),
        ],
        compiler_params=pltpu.CompilerParams(
            collective_id=0, has_side_effects=True, vmem_limit_bytes=40 * 2**20
        ),
    )(
        *(
            pltpu.with_memory_space_constraint(value, pltpu.HBM)
            for value in (
                v,
                counts,
                spin,
                flags.reshape((rounds, 2) + flags.shape[1:]),
                parity,
                displacement,
                heat,
            )
        )
    )
    return x * f[0]


def solution(mesh):
    sizes = (mesh.shape["bx"], mesh.shape["by"])
    cells = P(None, "bx", "by", None)
    return jax.shard_map(
        functools.partial(per_device, sizes),
        mesh=mesh,
        in_specs=(
            P(None, None, "bx", "by", None),
            P("bx", "by", None),
            cells,
            cells,
            P(),
            P(),
            P(),
        ),
        out_specs=P(None, None, "bx", "by", None),
        check_vma=False,
    )
```

```python
import functools
import math

import jax
import jax.numpy as jnp
from jax import lax
from jax.experimental import pallas as pl
from jax.experimental.pallas import tpu as pltpu
from jax.sharding import PartitionSpec as P

MESH = pl.DeviceIdType.MESH
AXES = ("bx", "by")
COS = math.cos(130.0 * math.pi / 180.0)
SIN = math.sin(130.0 * math.pi / 180.0)
EPSILON = 1e-06


def tree_sum(parts):
    parts = list(parts)
    while len(parts) > 1:
        parts = [sum(parts[i : i + 2]) for i in range(0, len(parts), 2)]
    return parts[0]


def column_sum(value):
    return jnp.sum(value, axis=0, keepdims=True)


def kernel(
    sizes,
    v_hbm,
    count_hbm,
    spin_hbm,
    flag_hbm,
    parity_hbm,
    displacement_hbm,
    heat_hbm,
    x_out,
    f_out,
    parity,
    displacement,
    heat,
    w,
    spin,
    flag_x,
    flag_y,
    flag_raw,
    count_x,
    count_y,
    p_x,
    p_y,
    p_z,
    p_tmp,
    iq_x,
    iq_y,
    rr_x,
    rr_y,
    closing,
    coupling,
    transfer,
    rows,
    load_sem,
    halo_send,
    halo_recv,
    row_send,
    row_recv,
    numbers,
    number_send,
    number_recv,
    total,
):
    n = sizes
    slots = v_hbm.shape[1]
    ex, ey, nz = count_hbm.shape
    extent = (ex, ey)
    rounds = spin_hbm.shape[0] // 2
    me = (lax.axis_index("bx"), lax.axis_index("by"))
    above = tuple(lax.rem(me[a] + 1, n[a]) for a in range(2))
    below = tuple(lax.rem(me[a] + n[a] - 1, n[a]) for a in range(2))
    my_row = me[0] * n[1] + me[1]
    columns = [me[0]]
    if n[0] % 2 == 0:
        half = n[0] // 2
        for i in range(half):
            for k in range(2):
                if i or k:
                    columns.append(
                        2 * lax.rem(me[0] // 2 + i, half) + lax.rem(lax.rem(me[0], 2) + k, 2)
                    )
    else:
        columns += [lax.rem(me[0] + i, n[0]) for i in range(1, n[0])]
    low_half = (2 * me[1]) // n[1] == 0
    peers = []
    for k in range(n[1] - 1):
        down = jnp.where(n[1] - 1 - k > me[1], n[1] - 1 - k, n[1] - 2 - k)
        up = jnp.where(k < me[1], k, k + 1)
        row = jnp.where(low_half, down, up)
        peers += [(column, row) for column in reversed(columns)]
    peers += [(column, me[1]) for column in reversed(columns[1:])]
    flag = (flag_x, flag_y)
    count = (count_x, count_y)
    mom = (p_x, p_y)
    iq = (iq_x, iq_y)
    rr = (rr_x, rr_y)

    load_count = pltpu.make_async_copy(count_hbm, count_x.at[pl.ds(1, ex)], load_sem.at[0])
    load_v = [pltpu.make_async_copy(v_hbm.at[c], w.at[c], load_sem.at[1 + c]) for c in range(3)]
    load_fx = pltpu.make_async_copy(flag_hbm.at[:, 0], flag_x.at[:, pl.ds(1, ex)], load_sem.at[4])
    load_fy = pltpu.make_async_copy(flag_hbm.at[:, 1], flag_raw, load_sem.at[5])
    load_spin = pltpu.make_async_copy(spin_hbm, spin, load_sem.at[6])
    load_scalars = [
        pltpu.make_async_copy(source, target, load_sem.at[7 + i])
        for i, (source, target) in enumerate(
            ((parity_hbm, parity), (displacement_hbm, displacement), (heat_hbm, heat))
        )
    ]
    for copy in load_scalars:
        copy.start()
    for copy in (load_count, load_v[0], load_fx, load_v[1], load_fy, load_v[2], load_spin):
        copy.start()

    barrier = pltpu.get_barrier_semaphore()
    for peer in peers:
        pl.semaphore_signal(barrier, inc=1, device_id=peer, device_id_type=MESH)

    def halo(view, a, kind):
        k = 2 * (2 * kind + a)
        return [
            pltpu.make_async_remote_copy(
                src_ref=view(extent[a]),
                dst_ref=view(0),
                send_sem=halo_send.at[k],
                recv_sem=halo_recv.at[k],
                device_id={AXES[a]: above[a]},
                device_id_type=MESH,
            ),
            pltpu.make_async_remote_copy(
                src_ref=view(1),
                dst_ref=view(extent[a] + 1),
                send_sem=halo_send.at[k + 1],
                recv_sem=halo_recv.at[k + 1],
                device_id={AXES[a]: below[a]},
                device_id_type=MESH,
            ),
        ]

    halo_p = [halo(lambda i, a=a: mom[a].at[i], a, 0) for a in range(2)]
    halo_c = [halo(lambda i, a=a: count[a].at[i], a, 1) for a in range(2)]
    halo_f = [halo(lambda i, a=a: flag[a].at[0, i], a, 2) for a in range(2)]
    halo_rest = [
        halo(lambda i, a=a: flag[a].at[pl.ds(1, rounds - 1), i], a, 3) for a in range(2)
    ]

    def start(copies):
        for copy in copies:
            copy.start()

    def finish(copies):
        for copy in copies:
            copy.wait()

    def inverse(counts):
        return 1.0 / jnp.maximum(counts.astype(jnp.float32), 1.0)

    def exchange(a, rows=rows, row_send=row_send, row_recv=row_recv):
        return [
            pltpu.make_async_remote_copy(
                src_ref=rows.at[a, my_row],
                dst_ref=rows.at[a, my_row],
                send_sem=row_send.at[a],
                recv_sem=row_recv.at[a],
                device_id=peer,
                device_id_type=MESH,
            )
            for peer in peers
        ]

    def await_rows(a, rows=rows, row_send=row_send, row_recv=row_recv):
        view = rows.at[a, pl.ds(0, n[0] * n[1] - 1)]
        whole = pltpu.make_async_remote_copy(
            src_ref=view,
            dst_ref=view,
            send_sem=row_send.at[a],
            recv_sem=row_recv.at[a],
            device_id=peers[0],
            device_id_type=MESH,
        )
        whole.wait_recv()
        whole.wait_send()

    def split_component(c, target, offset):
        def plane(i, acc):
            counts = count_x[i + 1]
            inv = iq_x[i + 1]
            values = [jnp.where(counts > s, w[c, s, i], 0.0) for s in range(slots)]
            moment = tree_sum(values)
            target[i + offset] = moment
            mean = moment * inv
            thermal = [jnp.where(counts > s, values[s] - mean, 0.0) for s in range(slots)]
            for s in range(slots):
                w[c, s, i] = thermal[s]
            heat_part = acc[0] + tree_sum([t * t for t in thermal])
            return heat_part, acc[1] + moment * mean

        zero = jnp.zeros((ey, nz), jnp.float32)
        return lax.fori_loop(0, ex, plane, (zero, zero))

    load_count.wait()
    number = jnp.zeros((ey, nz), jnp.float32)
    for i in range(1, ex + 1):
        iq_x[i] = inverse(count_x[i])
        number = number + count_x[i].astype(jnp.float32)
    load_v[0].wait()
    thermal_0, energy_x = split_component(0, p_x, 1)
    pl.semaphore_wait(barrier, n[0] * n[1] - 1)
    start(halo_p[0])
    start(halo_c[0])
    load_fx.wait()
    start(halo_f[0])
    numbers[0, my_row] = column_sum(number)
    start(exchange(0, numbers, number_send, number_recv))
    load_v[1].wait()
    thermal_1, energy_y = split_component(1, p_tmp, 0)
    for y in range(ey):
        p_y[y + 1] = p_tmp[:, y, :]
        count_y[y + 1] = count_x[pl.ds(1, ex), y, :]
    start(halo_p[1])
    start(halo_c[1])
    load_fy.wait()

    def flags_across(r, carry):
        for y in range(ey):
            flag_y[r, y + 1] = flag_raw[r, :, y, :]
        return carry

    lax.fori_loop(0, rounds, flags_across, 0)
    start(halo_f[1])
    load_v[2].wait()
    thermal_2, energy_z = split_component(2, p_z, 0)

    def reduced_masses(a):
        finish(halo_c[a])
        e = extent[a]
        for i in range(0, e + 2):
            iq[a][i] = inverse(count[a][i])
        for b in range(e + 1):
            low = count[a][b].astype(jnp.float32)
            high = count[a][b + 1].astype(jnp.float32)
            rr[a][b] = low * high / jnp.maximum(low + high, 1.0)

    def offset_of(a, t):
        return (me[a] * extent[a] - parity[t]) & 1

    def prepare(a, r, t, shift):
        finish(halo_p[a])
        p = offset_of(a, t)
        back = lax.rem(nz - shift, nz)
        for j in range((extent[a] + 1) // 2):
            low = 2 * j + 1 - p
            high = 2 * j + 2 - p
            closing[j] = jnp.maximum(
                mom[a][low] * iq[a][low] - mom[a][high] * iq[a][high], 0.0
            )
            outer = jnp.where(p == 0, flag[a][r, 2 * j + 2], flag[a][r, 2 * j])
            bits = jnp.maximum(flag[a][r, 2 * j + 1], outer).astype(jnp.float32)
            coupling[j] = pltpu.roll(bits, back, 1) * rr[a][low]

    def rotate(t, shift):
        back = lax.rem(nz - shift, nz)

        def plane(i, carry):
            kind = pltpu.roll(spin[t, i], back, 1)
            axis = kind >> 1
            sine = jnp.where((kind & 1) == 0, SIN, -SIN)
            own = [jnp.where(axis == c, 1.0, COS) for c in range(3)]
            sin = [jnp.where(axis == c, sine, 0.0) for c in range(3)]
            for s in range(slots):
                x, y, z = (w[c, s, i] for c in range(3))
                w[0, s, i] = own[0] * x + (sin[1] * z - sin[2] * y)
                w[1, s, i] = own[1] * y + (sin[2] * x - sin[0] * z)
                w[2, s, i] = own[2] * z + (sin[0] * y - sin[1] * x)
            return carry

        lax.fori_loop(0, ex, plane, 0)

    def collide(a, t, scale):
        p = offset_of(a, t)
        sign = (2 * p - 1).astype(jnp.float32)
        for j in range((extent[a] + 1) // 2):
            g = scale * closing[j]
            transfer[j] = coupling[j] * g * jnp.tanh(g)
        energy = []
        for i in range(1, extent[a] + 1):
            if i % 2 == 1:
                moved = scale * mom[a][i] + sign * transfer[(i - 1) // 2]
            else:
                moved = scale * mom[a][i] - sign * transfer[i // 2 - 1 + p]
            mom[a][i] = moved
            energy.append(moved * moved * iq[a][i])
        return column_sum(tree_sum(energy))

    load_spin.wait()
    for copy in load_scalars:
        copy.wait()
    reduced_masses(0)
    finish(halo_f[0])
    prepare(0, 0, 0, 0)
    ones = jnp.ones((1, nz), jnp.float32)

    def step(a, r, scales, energies, shift, last_hook):
        t = 2 * r + a
        b = 1 - a
        new_energy = collide(a, t, scales[a])
        partial = new_energy + energies[b] + energies[2]
        rows[a, my_row] = partial
        start(exchange(a))
        if a == 0:

            @pl.when(r > 0)
            def _():
                start(halo_p[1])

        else:

            @pl.when(r < rounds - 1)
            def _():
                start(halo_p[0])

        rotate(t, shift)
        if a == 0:

            @pl.when(r == 0)
            def _():
                start(halo_rest[0])
                start(halo_rest[1])
                reduced_masses(1)
                finish(halo_f[1])
                await_rows(0, numbers, number_send, number_recv)
                everyone = tree_sum([numbers[0, i] for i in range(n[0] * n[1])])
                everyone = jnp.sum(everyone, axis=1, keepdims=True)
                total[...] = jnp.broadcast_to(everyone, (1, nz))

        new_shift = lax.rem(shift + displacement[t], nz)
        if a == 0:
            prepare(1, r, t + 1, new_shift)
        else:

            @pl.when(r == 0)
            def _():
                finish(halo_rest[0])
                finish(halo_rest[1])

            @pl.when(r < rounds - 1)
            def _():
                prepare(0, r + 1, t + 1, new_shift)

            @pl.when(r == rounds - 1)
            def _():
                last_hook(scales, new_shift)

        root = jnp.sqrt((3.0 * heat[t]) * total[...])
        await_rows(a)
        sums = tree_sum([rows[a, i] for i in range(n[0] * n[1])])
        sums = jnp.sum(sums, axis=1, keepdims=True)
        kinetic = jnp.broadcast_to(sums, (1, nz))
        f = root * lax.rsqrt(kinetic + EPSILON)
        square = f * f
        kept = scales[b] * f
        scales = (f, kept, scales[2] * f) if a == 0 else (kept, f, scales[2] * f)
        moved = new_energy * square
        other = energies[b] * square
        pair = (moved, other) if a == 0 else (other, moved)
        return scales, pair + (energies[2] * square,), new_shift, f

    def assemble(scales, shift):
        for y in range(ey):
            p_tmp[:, y, :] = p_y[y + 1]

        def plane(i, carry):
            counts = count_x[i + 1]
            inv = iq_x[i + 1]
            means = (
                scales[0] * (p_x[i + 1] * inv),
                p_tmp[i] * inv,
                scales[2] * (p_z[i] * inv),
            )
            for c in range(3):
                for s in range(slots):
                    value = jnp.where(counts > s, means[c] + scales[2] * w[c, s, i], 0.0)
                    x_out[c, s, i] = pltpu.roll(value, shift, 1)
            return carry

        lax.fori_loop(0, ex, plane, 0)

    def round_body(r, carry):
        scales, energies, shift, _ = carry
        scales, energies, shift, f = step(0, r, scales, energies, shift, None)
        return step(1, r, scales, energies, shift, assemble)

    rest = column_sum(thermal_0 + thermal_1 + thermal_2 + energy_z)
    energies = (column_sum(energy_x), column_sum(energy_y), rest)
    carry = ((ones, ones, ones), energies, jnp.int32(0), ones)
    f_out[...] = lax.fori_loop(0, rounds, round_body, carry)[3]


def per_device(sizes, v, counts, spin, flags, parity, displacement, heat):
    slots = v.shape[1]
    ex, ey, nz = counts.shape
    steps = spin.shape[0]
    rounds = steps // 2
    bonds = (max(ex, ey) + 1) // 2
    assert ex % 2 == 1 and ey % 2 == 1 and ex == ey
    f32, i32 = jnp.float32, jnp.int32
    anywhere = pl.BlockSpec(memory_space=pltpu.HBM)
    vector = pl.BlockSpec(memory_space=pltpu.VMEM)
    dma = pltpu.SemaphoreType.DMA
    x, f = pl.pallas_call(
        functools.partial(kernel, sizes),
        out_shape=(
            jax.ShapeDtypeStruct(v.shape, f32),
            jax.ShapeDtypeStruct((1, nz), f32),
        ),
        in_specs=[anywhere] * 7,
        out_specs=(vector, vector),
        scratch_shapes=[
            pltpu.SMEM(parity.shape, i32),
            pltpu.SMEM(displacement.shape, i32),
            pltpu.SMEM(heat.shape, f32),
            pltpu.VMEM(v.shape, f32),
            pltpu.VMEM(spin.shape, i32),
            pltpu.VMEM((rounds, ex + 2, ey, nz), i32),
            pltpu.VMEM((rounds, ey + 2, ex, nz), i32),
            pltpu.VMEM((rounds, ex, ey, nz), i32),
            pltpu.VMEM((ex + 2, ey, nz), i32),
            pltpu.VMEM((ey + 2, ex, nz), i32),
            pltpu.VMEM((ex + 2, ey, nz), f32),
            pltpu.VMEM((ey + 2, ex, nz), f32),
            pltpu.VMEM((ex, ey, nz), f32),
            pltpu.VMEM((ex, ey, nz), f32),
            pltpu.VMEM((ex + 2, ey, nz), f32),
            pltpu.VMEM((ey + 2, ex, nz), f32),
            pltpu.VMEM((ex + 1, ey, nz), f32),
            pltpu.VMEM((ey + 1, ex, nz), f32),
            pltpu.VMEM((bonds, ey, nz), f32),
            pltpu.VMEM((bonds, ey, nz), f32),
            pltpu.VMEM((bonds, ey, nz), f32),
            pltpu.VMEM((2, sizes[0] * sizes[1], 1, nz), f32),
            dma((10,)),
            dma((16,)),
            dma((16,)),
            dma((2,)),
            dma((2,)),
            pltpu.VMEM((1, sizes[0] * sizes[1], 1, nz), f32),
            dma((1,)),
            dma((1,)),
            pltpu.VMEM((1, nz), f32),
        ],
        compiler_params=pltpu.CompilerParams(
            collective_id=0, has_side_effects=True, vmem_limit_bytes=40 * 2**20
        ),
    )(
        *(
            pltpu.with_memory_space_constraint(value, pltpu.HBM)
            for value in (
                v,
                counts,
                spin,
                flags.reshape((rounds, 2) + flags.shape[1:]),
                parity,
                displacement,
                heat,
            )
        )
    )
    return x * f[0]


def solution(mesh):
    sizes = (mesh.shape["bx"], mesh.shape["by"])
    cells = P(None, "bx", "by", None)
    return jax.shard_map(
        functools.partial(per_device, sizes),
        mesh=mesh,
        in_specs=(
            P(None, None, "bx", "by", None),
            P("bx", "by", None),
            cells,
            cells,
            P(),
            P(),
            P(),
        ),
        out_specs=P(None, None, "bx", "by", None),
        check_vma=False,
    )
```
